128 devices in a mesh: dp: 32 (over z, x_hi, y), own: 4 (over x_lo, core).
Axes of the slice: x: 4 (x_hi: 2, x_lo: 2; x = x_hi * 2 + x_lo), y: 4, z: 4, core: 2. Of those that a mesh axis runs over, the one named last changes fastest.
Arguments:
- tokens: bfloat16 [4096, 6144], P('dp', 'own'), may hold values from -6 to 6
- expert_ids: int32 [4096, 2], P('dp'), may hold values from 0 to 7, all different within a row; in each aligned block of 128 rows (0 to 127, 128 to 255, ...) at most 40 rows name the same one
- combine_weights: float32 [4096, 2], P('dp'), may hold values from 0.2 to 1
- gate_weight: bfloat16 [2, 6144, 8192], P(None, 'own', 'dp'), may hold values from -0.078125 to 0.078125
- up_weight: bfloat16 [2, 6144, 8192], P(None, 'own', 'dp'), may hold values from -0.078125 to 0.078125
- down_weight: bfloat16 [2, 8192, 6144], P(None, 'dp', 'own'), may hold values from -0.0625 to 0.0625
- out_grad: bfloat16 [4096, 6144], P('dp', 'own'), may hold values from -6 to 6
Outputs:
- mixed: bfloat16 [4096, 6144], P('dp', 'own')
- token_grad: bfloat16 [4096, 6144], P('dp', 'own')
- gate_grad_weight: float32 [2, 6144, 8192], P(None, 'own', 'dp')
- up_grad_weight: float32 [2, 6144, 8192], P(None, 'own', 'dp')
- down_grad_weight: float32 [2, 8192, 6144], P(None, 'dp', 'own')
The draws below stay inside these ranges and needn't reach their ends.
Inputs may be any that keep to these rules, and one draw needn't show every extreme that they name: `expert_ids`: each row names 2 different experts. The 128 rows of one index of dp name each expert at most 40 times, and in every draw some expert is named exactly 40 times by the rows of one index of dp.
All inputs are finite; a program needn't handle non-finite values.
Results may differ from the reference program's by a relative error of at most 0.024.
Values may be sent and summed in bfloat16 or wider, within the bound.
A program may use at most 192 MiB of HBM per device.

```python
import math
import jax
import jax.numpy as jnp
import numpy as np
from jax import lax

D = 6144
FF = 8192
NEXP = 8
TOPK = 2
E = 2
TOK_DEV = 128
CAP = 40
TOKENS = 4096
N_DP = 32
N_OWN = 4


def level_of(stream_key, dims, cuts, smallest, high):
    def one(dim, blocks):
        heights = jax.random.uniform(jax.random.fold_in(jax.random.fold_in(stream_key, 6), dim), (blocks,), jnp.float32, smallest / len(cuts), high / len(cuts))
        return jnp.repeat(jnp.exp(heights), dims[dim] // blocks).reshape((-1,) + (1,) * (len(dims) - dim - 1))

    factor_of = one(*cuts[0])
    for cut in cuts[1:]:
        factor_of = factor_of * one(*cut)
    return factor_of


def shared_out(own_key, own, number, rows, count, top, bound, slope):
    order = jax.random.permutation(own_key, count)
    heavy_load, common = load_shares(count, rows * top, bound, slope, True), load_shares(count, rows * top, bound, slope, False)
    places = jnp.arange(count)

    def named(sizes, rotation):
        used = int((sizes > 0).sum())
        fixed = max(1, used // 4)
        shifted = fixed + (places - fixed + rotation * (used - fixed)) % max(1, count - fixed)
        return jnp.zeros((count,), jnp.int32).at[order[jnp.where(places < fixed, places, shifted)]].set(jnp.asarray(sizes, jnp.int32))

    sizes = jnp.where(number % 4 == 0, named(heavy_load, number // 4), named(common, number - number // 4 - 1))
    mixed = jax.random.permutation(jax.random.fold_in(own, 3), count)
    donor, sink = mixed[0:count // 2 * 2:2], mixed[1:count // 2 * 2:2]
    slack = jnp.minimum(sizes[donor] - 1, bound - sizes[sink]) // 2
    slack = jnp.where((donor == order[0]) | (sink == order[0]) | (sizes[sink] == 0), 0, jnp.maximum(slack, 0))
    shifted = jax.random.randint(jax.random.fold_in(own, 4), (count // 2,), 0, 1 << 20) % (slack + 1)
    sizes = sizes.at[donor].add(-shifted).at[sink].add(shifted)
    members = jnp.searchsorted(jnp.cumsum(sizes), jnp.arange(rows * top), side="right").astype(jnp.int32)
    listing = members.reshape(top, rows).T
    listing = listing[jax.random.permutation(jax.random.fold_in(own, 1), rows)]
    rotation = jax.random.randint(jax.random.fold_in(own, 2), (rows, 1), 0, top)
    return jnp.take_along_axis(listing, (jnp.arange(top)[None, :] + rotation) % top, axis=1)


def load_shares(count, total, most, skew, full):
    weights = [(1 << 20) // math.isqrt(rank ** skew) + 1 for rank in range(1, count + 1)]
    largest = most if full else min(most, max(-(-total // count), total * weights[0] // sum(weights)))
    least = 1 if total - largest >= count - 1 else 0
    counts, spare = [largest] + [least] * (count - 1), total - largest - least * (count - 1)
    while spare > 0:
        candidates = [i for i in range(1, count) if counts[i] < largest] or [i for i in range(1, count) if counts[i] < most]
        whole, budget = sum([weights[i] for i in candidates]), spare
        for i in candidates:
            more = min(most - counts[i], max(1, budget * weights[i] // whole), spare)
            counts[i] = counts[i] + more
            spare = spare - more
    return np.array(counts)


def gaussian(rng, dims, scale, reach, cuts=(), held_as=jnp.bfloat16):
    gain = level_of(rng, dims, cuts, -0.22, 0.18) if cuts else 1.0
    values = jax.random.normal(rng, dims, jnp.float32) * scale * gain
    return jnp.minimum(jnp.maximum(values, -reach), reach).astype(held_as)


def setup_inputs(seed: int = 0) -> dict:
    seeds = jax.random.split(jax.random.key(seed), 8)
    tokens = gaussian(seeds[0], (TOKENS, D), 1.0, 6.0, ((0, 32), (1, 4)))
    expert_ids_keys = jax.random.split(jax.random.fold_in(seeds[1], 1), TOKENS // TOK_DEV)
    expert_ids_turns = jax.random.permutation(jax.random.fold_in(seeds[1], 3), TOKENS // TOK_DEV)
    expert_ids = jax.vmap(lambda own, number: shared_out(jax.random.fold_in(seeds[1], 2), own, number, TOK_DEV, NEXP, TOPK, CAP, 1))(expert_ids_keys, expert_ids_turns).reshape((TOKENS, TOPK))
    combine_weights = jnp.clip(0.2 + 0.8 * jax.random.uniform(seeds[2], (TOKENS, TOPK), jnp.float32) ** level_of(seeds[2], (TOKENS, TOPK), ((0, 32),), -0.2, 0.2), 0.2, 1.0)
    gate_weight = gaussian(seeds[3], (E, D, FF), D ** -0.5, 0.078125, ((1, 4), (2, 32)))
    up_weight = gaussian(seeds[4], (E, D, FF), D ** -0.5, 0.078125, ((1, 4), (2, 32)))
    down_weight = gaussian(seeds[5], (E, FF, D), FF ** -0.5, 0.0625, ((1, 32), (2, 4)))
    out_grad = gaussian(seeds[6], (TOKENS, D), 1.0, 6.0, ((0, 32), (1, 4)))
    return dict(tokens=tokens, expert_ids=expert_ids, combine_weights=combine_weights, gate_weight=gate_weight, up_weight=up_weight, down_weight=down_weight, out_grad=out_grad)


def slot_order(shard_ids, expert):
    chosen = shard_ids == expert
    routed = jnp.any(chosen, axis=-1)
    position = (jnp.cumsum(routed.astype(jnp.int32)) - 1).astype(jnp.int32)
    slot_ids = jnp.arange(CAP, dtype=jnp.int32)
    matches = routed[None, :] & (position[None, :] == slot_ids[:, None])
    token_ids = jnp.arange(shard_ids.shape[0], dtype=jnp.int32)
    source = jnp.sum(jnp.where(matches, token_ids[None, :], 0), axis=1).astype(jnp.int32)
    filled = jnp.any(matches, axis=1)
    target = jnp.where(routed, position, 0).astype(jnp.int32)
    return chosen, routed, source, filled, target


def tables_for(expert_ids, combine_weights, expert):
    shards = expert_ids.reshape(N_DP, TOK_DEV, TOPK)

    def one_shard(shard_ids):
        return slot_order(shard_ids, expert)

    chosen, routed, source, filled, target = jax.vmap(one_shard)(shards)
    shard_base = jnp.arange(N_DP, dtype=jnp.int32)
    source = (source + shard_base[:, None] * TOK_DEV).astype(jnp.int32).reshape(-1)
    target = (target + shard_base[:, None] * CAP).astype(jnp.int32).reshape(-1)
    weight = jnp.sum(jnp.where(chosen.reshape(-1, TOPK), combine_weights, 0.0), axis=-1)
    return routed.reshape(-1), source, filled.reshape(-1), target, weight


def own_blocks(left, right):
    row_total = left.shape[0]
    left_blocks = left.astype(jnp.float32).reshape(row_total, N_OWN, D // N_OWN)
    right_blocks = right.astype(jnp.float32).reshape(N_OWN, D // N_OWN, right.shape[1])
    partial_sums = jnp.einsum("rjd,jdf->jrf", left_blocks, right_blocks).astype(jnp.bfloat16)
    partial_sums = lax.optimization_barrier(partial_sums)
    return jnp.sum(partial_sums.astype(jnp.float32), axis=0)


def dp_blocks(lefts, rights):
    row_total = lefts[0].shape[0]
    width = rights[0].shape[1]
    left_blocks = tuple(item.reshape(row_total, N_DP, FF // N_DP).transpose(1, 0, 2) for item in lefts)
    right_blocks = tuple(item.reshape(N_DP, FF // N_DP, width) for item in rights)

    def step(carry, pieces):
        left_pieces, right_pieces = pieces
        block_sum = jnp.zeros((row_total, width), jnp.float32)
        for left_item, right_item in zip(left_pieces, right_pieces):
            block_sum = block_sum + jnp.dot(left_item, right_item, preferred_element_type=jnp.float32)
        rounded = lax.optimization_barrier(block_sum.astype(jnp.bfloat16))
        return carry + rounded.astype(jnp.float32), None

    result, unused = lax.scan(step, jnp.zeros((row_total, width), jnp.float32), (left_blocks, right_blocks))
    return result


def reference(tokens, expert_ids, combine_weights, gate_weight, up_weight, down_weight, out_grad):
    mixed = jnp.zeros((TOKENS, D), jnp.float32)
    token_grad = jnp.zeros((TOKENS, D), jnp.float32)
    gate_grads = []
    up_grads = []
    down_grads = []
    for expert in range(E):
        routed, source, filled, target, weight = tables_for(expert_ids, combine_weights, expert)
        dispatched = jnp.where(filled[:, None], tokens[source], 0).astype(jnp.bfloat16)
        gate_sum = own_blocks(dispatched, gate_weight[expert])
        up_sum = own_blocks(dispatched, up_weight[expert])
        sigma = jax.nn.sigmoid(gate_sum)
        swish = gate_sum * sigma
        hidden = (swish * up_sum).astype(jnp.bfloat16)
        expert_out = dp_blocks((hidden,), (down_weight[expert],))
        token_weight = jnp.where(routed, weight, 0.0)
        mixed = mixed + token_weight[:, None] * expert_out[target]
        slot_weight = jnp.where(filled, weight[source], 0.0)
        scaled = (slot_weight[:, None] * out_grad[source].astype(jnp.float32)).astype(jnp.bfloat16)
        hidden_grad = own_blocks(scaled, down_weight[expert].T)
        gate_grad = (hidden_grad * up_sum * sigma * (1.0 + gate_sum * (1.0 - sigma))).astype(jnp.bfloat16)
        up_grad = (hidden_grad * swish).astype(jnp.bfloat16)
        row_grad = dp_blocks((gate_grad, up_grad), (gate_weight[expert].T, up_weight[expert].T))
        token_grad = token_grad + jnp.where(routed[:, None], row_grad[target], 0.0)
        gate_grads.append(jnp.dot(dispatched.T, gate_grad, preferred_element_type=jnp.float32))
        up_grads.append(jnp.dot(dispatched.T, up_grad, preferred_element_type=jnp.float32))
        down_grads.append(jnp.dot(hidden.T, scaled, preferred_element_type=jnp.float32))
    return (mixed.astype(jnp.bfloat16), token_grad.astype(jnp.bfloat16),
            jnp.stack(gate_grads), jnp.stack(up_grads), jnp.stack(down_grads))
```

```python
import jax
import jax.numpy as jnp
from jax import lax
from jax.experimental import pallas as pl
from jax.experimental.pallas import tpu as pltpu
from jax.sharding import PartitionSpec as P

CAP = 40
RING = 4
CHUNK = RING * CAP
HALF = CHUNK // 2
TILE = 256
MESH = pl.DeviceIdType.MESH
F32 = jnp.float32
BF16 = jnp.bfloat16
MESSAGES = ((0, 1, 0), (1, 1, 0), (0, -1, 0), (1, -1, 0), (0, 1, -1), (1, -1, 1))


def dp_of(z, x, y):
    return z * 8 + x * 4 + y


def place():
    dp, own = lax.axis_index("dp"), lax.axis_index("own")
    z, x, y = dp // 8, (dp // 4) % 2, dp % 4
    core, low = own % 2, own // 2

    def along(axis, step):
        if axis == "y":
            return (dp_of(z, x, (y + step + RING) % RING), own)
        return (dp_of((z + step + RING) % RING, x, y), own)

    partner = (dp_of(z, 1 - x, y), own)
    sibling = (dp, low * 2 + (1 - core))
    across = (dp, (1 - low) * 2 + core)
    return z, x, y, core, along, partner, sibling, across


def send(src, dst, send_sem, recv_sem, device):
    return pltpu.make_async_remote_copy(
        src_ref=src, dst_ref=dst, send_sem=send_sem, recv_sem=recv_sem, device_id=device, device_id_type=MESH
    )


def meet(devices):
    barrier = pltpu.get_barrier_semaphore()
    for device in devices:
        pl.semaphore_signal(barrier, inc=1, device_id=device, device_id_type=MESH)
    return barrier, len(devices)


def nt(a, b):
    return lax.dot_general(a, b, (((1,), (1,)), ((), ())), preferred_element_type=F32)


def nn(a, b):
    return jnp.dot(a, b, preferred_element_type=F32)


def tn(a, b):
    return lax.dot_general(a, b, (((0,), (0,)), ((), ())), preferred_element_type=F32)


def layer_kernel(
    tok, ids, mix, grad, wg_h, wu_h, wd_h,
    mixed, token_grad, dg_h, du_h, dd_h, x_all,
    mine, hot, wg, wu, wd, xin, part, r1, s1, r2, act,
    pb, rd, rb, s2, td, tb, ts, x3, rx3, win, wout,
    load_sem, put_sem, xin_sem, win_sem, wout_sem,
    ag_send, ag_recv, x_send, x_recv, own_send, own_recv, c_send, c_recv, y_send, y_recv,
):
    z, x, y, core, along, partner, sibling, across = place()
    first, second = ("y", "z"), ("z", "y")
    coord = {"y": y, "z": z}
    width = wd.shape[-1]
    tiles = width // TILE
    loads = [
        pltpu.make_async_copy(src, dst, load_sem.at[i])
        for i, (src, dst) in enumerate(((wg_h, wg), (wu_h, wu), (wd_h, wd)))
    ]
    for load in loads:
        load.start()
    barrier, count = meet(
        (along("y", 1), along("y", -1), along("z", 1), along("z", -1), partner, sibling, across)
    )
    shard = tok.shape[0]
    earlier = lax.broadcasted_iota(jnp.int32, (shard, shard), 1) < lax.broadcasted_iota(
        jnp.int32, (shard, shard), 0
    )
    slots = lax.broadcasted_iota(jnp.int32, (shard, CAP), 1).astype(F32)
    weight = []
    for e in range(2):
        chosen = (ids[...] == e).astype(F32)
        routed = jnp.sum(chosen, axis=1, keepdims=True)
        weight.append(jnp.sum(chosen * mix[...], axis=1, keepdims=True))
        spread = jnp.broadcast_to(routed, (shard, 128)).astype(BF16)
        position = nn(earlier.astype(F32).astype(BF16), spread)[:, 0:1]
        hot[e] = jnp.where((routed > 0.0) & (position == slots), 1.0, 0.0).astype(BF16)
        mine[0, e] = tn(hot[e], tok[...]).astype(BF16)
        mine[1, e] = tn(hot[e], (weight[e] * grad[...].astype(F32)).astype(BF16)).astype(BF16)
    pl.semaphore_wait(barrier, count)

    def plane(wave):
        return x if wave == 0 else 1 - x

    def q_of(e):
        return z + e * (y - z)

    def piece(t, e, xs, qc, pc):
        row = pl.multiple_of((xs * 16 + qc * 4 + pc) * CAP, 8)
        return x_all.at[t, e, pl.ds(row, CAP)]

    def chunk(t, e, xs, qc):
        row = pl.multiple_of((xs * 4 + qc) * CHUNK, 32)
        return x_all.at[t, e, pl.ds(row, CHUNK)]

    def phase(wave, e, stage, m, arriving=False):
        t, way, shift = MESSAGES[m]
        axis = (first if stage == 0 else second)[e]
        a, b, xs = coord[first[e]], coord[second[e]], plane(wave)
        if arriving:
            shift = shift - way
        if stage == 0:
            ref = piece(t, e, xs, b, (a + shift + RING) % RING)
            src = mine.at[t, e] if wave == 0 and m < 4 and not arriving else ref
        else:
            ref = chunk(t, e, xs, (b + shift + RING) % RING)
            src = ref
        index = ((wave * 2 + e) * 2 + stage) * 6 + m
        return send(src, ref, ag_send.at[index], ag_recv.at[index], along(axis, way))

    def start(wave, stage, messages):
        for m in messages:
            for e in range(2):
                phase(wave, e, stage, m).start()

    def arrive(wave, stage, messages):
        for m in messages:
            for e in range(2):
                phase(wave, e, stage, m, True).wait_recv()

    def relay(wave, stage):
        for came, out in ((0, 4), (3, 5)):
            arrive(wave, stage, (came,))
            start(wave, stage, (out,))

    puts, crossings, landings = [], [], []
    for t in range(2):
        for e in range(2):
            a, b, i = coord[first[e]], coord[second[e]], t * 2 + e
            puts.append(pltpu.make_async_copy(mine.at[t, e], piece(t, e, x, b, a), put_sem.at[i]))
            crossings.append(send(mine.at[t, e], piece(t, e, x, b, a), x_send.at[i], x_recv.at[i], partner))
            theirs = piece(t, e, 1 - x, b, a)
            landings.append(send(mine.at[t, e], theirs, x_send.at[i], x_recv.at[i], partner))

    steps = [(wave, shift) for wave in range(2) for shift in (0, -1, 1, 2)]

    def row_of(e, wave, shift):
        return (plane(wave) * 4 + (q_of(e) + shift + RING) % RING) * CHUNK

    def own_one(step, e):
        i = step * 2 + e
        far = pl.multiple_of((1 - core) * HALF, HALF)
        return send(part.at[i, :, pl.ds(far, HALF)], r1.at[i], own_send.at[i], own_recv.at[i], sibling)

    def own_two(step, e):
        i = step * 2 + e
        return send(s1.at[i], r2.at[i], own_send.at[16 + i], own_recv.at[16 + i], across)

    def own_three(step, e, arriving=False):
        i = step * 2 + e
        wave, shift = steps[step]
        side = 1 - core if arriving else core
        row = pl.multiple_of(row_of(e, wave, shift) + side * HALF, 16)
        ref = act.at[:, e, pl.ds(row, HALF)]
        return send(ref, ref, own_send.at[32 + i], own_recv.at[32 + i], sibling)

    def fetch(step):
        wave, shift = steps[step]
        return [
            pltpu.make_async_copy(
                chunk(t, e, plane(wave), (q_of(e) + shift + RING) % RING), xin.at[t, e], xin_sem.at[t * 2 + e]
            )
            for t in range(2)
            for e in range(2)
        ]

    def matmuls(step):
        def one(e, carry):
            i = step * 2 + e
            part[i, 0] = nn(xin[0, e], wg[e]).astype(BF16)
            part[i, 1] = nn(xin[0, e], wu[e]).astype(BF16)
            part[i, 2] = nt(xin[1, e], wd[e]).astype(BF16)
            own_one(step, e).start()
            return carry

        lax.fori_loop(0, 2, one, 0)

    def halves(step):
        def one(e, carry):
            i = step * 2 + e
            own_one(step, e).wait_recv()
            near = pl.multiple_of(core * HALF, HALF)
            for k in range(3):
                total = part[i, k, pl.ds(near, HALF), :].astype(F32) + r1[i, k].astype(F32)
                s1[i, k] = total.astype(BF16)
            own_two(step, e).start()
            return carry

        lax.fori_loop(0, 2, one, 0)

    def gates(step):
        wave, shift = steps[step]

        def one(e, carry):
            i = step * 2 + e
            own_two(step, e).wait_recv()
            row = pl.multiple_of(row_of(e, wave, shift) + core * HALF, 16)
            gate = s1[i, 0].astype(F32) + r2[i, 0].astype(F32)
            up = s1[i, 1].astype(F32) + r2[i, 1].astype(F32)
            back = s1[i, 2].astype(F32) + r2[i, 2].astype(F32)
            sigma = jax.nn.sigmoid(gate)
            swish = gate * sigma
            act[0, e, pl.ds(row, HALF), :] = (swish * up).astype(BF16)
            act[1, e, pl.ds(row, HALF), :] = (back * up * sigma * (1.0 + gate * (1.0 - sigma))).astype(BF16)
            act[2, e, pl.ds(row, HALF), :] = (back * swish).astype(BF16)
            own_three(step, e).start()
            return carry

        lax.fori_loop(0, 2, one, 0)

    def compute(step):
        copies = fetch(step)
        for copy in copies:
            copy.start()
        if step >= 2:
            gates(step - 2)
        for copy in copies:
            copy.wait()
        matmuls(step)
        if step >= 1:
            halves(step - 1)

    def settled(group):
        for step in group:
            for e in range(2):
                own_three(step, e, True).wait_recv()

    def hop(side, e, stage, m):
        t = m % 2
        way = (1, -1, 1, -1, -1, 1)[m]
        axis = (second if stage == 0 else first)[e]
        index = ((side * 2 + e) * 2 + stage) * 6 + m
        if stage == 0:
            src = pb.at[side, (3, 3, 1, 2, 2, 1)[m], t, e]
            dst = rd.at[side, t, e] if m < 2 else rb.at[side, (m - 2) // 2, t, e]
        else:
            a = coord[first[e]]
            far = s2.at[side, t, e, (a + 2) % RING]
            near = s2.at[side, t, e, (a + way + RING) % RING]
            src = far if m < 2 else ts.at[side, t, e] if m < 4 else near
            dst = td.at[side, t, e] if m < 2 else tb.at[side, (m - 2) // 2, t, e]
        return send(src, dst, c_send.at[index], c_recv.at[index], along(axis, way))

    def go(side, stage, messages):
        for m in messages:
            for e in range(2):
                hop(side, e, stage, m).start()

    def come(side, stage, messages):
        for m in messages:
            for e in range(2):
                hop(side, e, stage, m).wait_recv()

    def over_tiles(one):
        def step(i, carry):
            e, n = i // tiles, i % tiles
            one(e, pl.ds(pl.multiple_of(n * TILE, TILE), TILE))
            return carry

        lax.fori_loop(0, 2 * tiles, step, 0)

    def produce(side, j):
        shift = (0, 1, -1, 2)[j]

        def one(e, col):
            rows = pl.ds(pl.multiple_of(row_of(e, 1 - side, shift), 32), CHUNK)
            pb[side, j, 0, e, :, col] = nn(act[0, e, rows, :], wd[e, :, col]).astype(BF16)
            back = nt(act[1, e, rows, :], wg[e, col, :]) + nt(act[2, e, rows, :], wu[e, col, :])
            pb[side, j, 1, e, :, col] = back.astype(BF16)

        over_tiles(one)

    def relay_first(side):
        for t in range(2):
            come(side, 0, (t,))

            def one(e, col):
                total = pb[side, 1 + t, t, e, :, col].astype(F32) + rd[side, t, e, :, col].astype(F32)
                pb[side, 1 + t, t, e, :, col] = total.astype(BF16)

            over_tiles(one)
            go(side, 0, (2 + t,))

    def gather_first(side):
        come(side, 0, (2, 3, 4, 5))
        for t in range(2):

            def one(e, col):
                total = (
                    pb[side, 0, t, e, :, col].astype(F32)
                    + rb[side, 0, t, e, :, col].astype(F32)
                    + rb[side, 1, t, e, :, col].astype(F32)
                )
                for k in range(RING):
                    s2[side, t, e, k, :, col] = total[k * CAP : (k + 1) * CAP].astype(BF16)

            over_tiles(one)
        go(side, 1, (0, 1, 4, 5))

    def relay_second(side):
        for t in range(2):
            come(side, 1, (t,))
            for e in range(2):
                a = coord[first[e]]
                near = (a + (1, -1)[t] + RING) % RING
                total = s2[side, t, e, near].astype(F32) + td[side, t, e].astype(F32)
                ts[side, t, e] = total.astype(BF16)
            go(side, 1, (2 + t,))

    def total_second(side, t, e):
        a = coord[first[e]]
        return (
            s2[side, t, e, a].astype(F32)
            + tb[side, 0, t, e].astype(F32)
            + tb[side, 1, t, e].astype(F32)
        )

    def crossing(t, e):
        i = t * 2 + e
        return send(x3.at[t, e], rx3.at[t, e], y_send.at[i], y_recv.at[i], partner)

    def weight_in(i, slot):
        e, n = i // tiles, i % tiles
        col = pl.ds(pl.multiple_of(n * TILE, TILE), TILE)
        return [
            pltpu.make_async_copy(x_all.at[t, e, :, col], win.at[slot, t], win_sem.at[slot, t]) for t in range(2)
        ]

    def weight_out(i, slot):
        e, n = i // tiles, i % tiles
        col = pl.ds(pl.multiple_of(n * TILE, TILE), TILE)
        return [
            pltpu.make_async_copy(wout.at[slot, 0], dg_h.at[e, col], wout_sem.at[slot, 0]),
            pltpu.make_async_copy(wout.at[slot, 1], du_h.at[e, col], wout_sem.at[slot, 1]),
            pltpu.make_async_copy(wout.at[slot, 2], dd_h.at[e, :, col], wout_sem.at[slot, 2]),
        ]

    last = 2 * tiles

    def weight_grads(begin, end):
        def step(i, carry):
            slot = i % 2
            for copy in weight_in(i, slot):
                copy.wait()

            @pl.when(i + 1 < last)
            def _():
                for copy in weight_in(i + 1, 1 - slot):
                    copy.start()

            @pl.when(i >= 2)
            def _():
                for copy in weight_out(i - 2, slot):
                    copy.wait()

            e = i // tiles
            wout[slot, 0] = tn(win[slot, 0], act[1, e])
            wout[slot, 1] = tn(win[slot, 0], act[2, e])
            wout[slot, 2] = tn(act[0, e], win[slot, 1])
            for copy in weight_out(i, slot):
                copy.start()
            return carry

        lax.fori_loop(begin, end, step, 0)

    order = (0, 3, 1, 2)
    start(0, 0, order)
    for copy in crossings + puts:
        copy.start()
    relay(0, 0)
    arrive(0, 0, (1, 2, 4, 5))
    for copy in puts:
        copy.wait()
    start(0, 1, order)
    for copy in landings:
        copy.wait_recv()
    start(1, 0, order)
    for load in loads:
        load.wait()
    compute(0)
    relay(1, 0)
    relay(0, 1)
    arrive(1, 0, (1, 2, 4, 5))
    start(1, 1, order)
    arrive(0, 1, (1,))
    compute(1)
    arrive(0, 1, (2,))
    compute(2)
    arrive(0, 1, (4, 5))
    compute(3)
    compute(4)
    relay(1, 1)
    arrive(1, 1, (1,))
    compute(5)
    arrive(1, 1, (2,))
    compute(6)
    settled((0, 1, 2, 3))
    produce(1, 3)
    produce(1, 1)
    produce(1, 2)
    produce(1, 0)
    arrive(1, 1, (4, 5))
    go(1, 0, (0, 1, 5, 4))
    compute(7)
    gates(6)
    halves(7)
    for copy in weight_in(0, 0):
        copy.start()
    gates(7)
    settled((4, 5, 6, 7))
    produce(0, 3)
    go(0, 0, (0, 1))
    produce(0, 1)
    go(0, 0, (5,))
    produce(0, 2)
    go(0, 0, (4,))
    produce(0, 0)
    weight_grads(0, 4)
    relay_first(0)
    relay_first(1)
    weight_grads(4, 8)
    gather_first(0)
    weight_grads(8, 10)
    relay_second(0)
    weight_grads(10, last)
    come(0, 1, (2, 3, 4, 5))
    for t in range(2):
        for e in range(2):
            x3[t, e] = total_second(0, t, e).astype(BF16)
            crossing(t, e).start()
    gather_first(1)
    relay_second(1)
    come(1, 1, (2, 3, 4, 5))
    final = [[None, None], [None, None]]
    for t in range(2):
        for e in range(2):
            crossing(t, e).wait_recv()
            final[t][e] = (total_second(1, t, e) + rx3[t, e].astype(F32)).astype(BF16)
    mixed[...] = (weight[0] * nn(hot[0], final[0][0]) + weight[1] * nn(hot[1], final[0][1])).astype(BF16)
    token_grad[...] = (nn(hot[0], final[1][0]) + nn(hot[1], final[1][1])).astype(BF16)
    for i in (last - 2, last - 1):
        for copy in weight_out(i, i % 2):
            copy.wait()
    for e in range(2):
        for wave in range(2):
            for stage in range(2):
                for m in range(6):
                    phase(wave, e, stage, m).wait_send()
                    hop(wave, e, stage, m).wait_send()
        for t in range(2):
            crossings[t * 2 + e].wait_send()
            crossing(t, e).wait_send()
        for step in range(8):
            own_one(step, e).wait_send()
            own_two(step, e).wait_send()
            own_three(step, e).wait_send()


def local(tokens, expert_ids, combine_weights, gate_weight, up_weight, down_weight, out_grad):
    shard, width = tokens.shape
    experts, hidden = gate_weight.shape[0], gate_weight.shape[2]
    rows = 32 * CAP
    vmem = pl.BlockSpec(memory_space=pltpu.VMEM)
    hbm = pl.BlockSpec(memory_space=pl.ANY)
    dma = pltpu.SemaphoreType.DMA
    out = jax.ShapeDtypeStruct((shard, width), BF16)
    result = pl.pallas_call(
        layer_kernel,
        out_shape=(
            out,
            out,
            jax.ShapeDtypeStruct(gate_weight.shape, F32),
            jax.ShapeDtypeStruct(up_weight.shape, F32),
            jax.ShapeDtypeStruct(down_weight.shape, F32),
            jax.ShapeDtypeStruct((2, experts, rows, width), BF16),
        ),
        in_specs=[vmem] * 4 + [hbm] * 3,
        out_specs=(vmem,) * 2 + (hbm,) * 4,
        scratch_shapes=[
            pltpu.VMEM((2, 2, CAP, width), BF16),
            pltpu.VMEM((2, shard, CAP), BF16),
            pltpu.VMEM(gate_weight.shape, BF16),
            pltpu.VMEM(up_weight.shape, BF16),
            pltpu.VMEM(down_weight.shape, BF16),
            pltpu.VMEM((2, 2, CHUNK, width), BF16),
            pltpu.VMEM((16, 3, CHUNK, hidden), BF16),
            pltpu.VMEM((16, 3, HALF, hidden), BF16),
            pltpu.VMEM((16, 3, HALF, hidden), BF16),
            pltpu.VMEM((16, 3, HALF, hidden), BF16),
            pltpu.VMEM((3, 2, rows, hidden), BF16),
            pltpu.VMEM((2, 4, 2, 2, CHUNK, width), BF16),
            pltpu.VMEM((2, 2, 2, CHUNK, width), BF16),
            pltpu.VMEM((2, 2, 2, 2, CHUNK, width), BF16),
            pltpu.VMEM((2, 2, 2, RING, CAP, width), BF16),
            pltpu.VMEM((2, 2, 2, CAP, width), BF16),
            pltpu.VMEM((2, 2, 2, 2, CAP, width), BF16),
            pltpu.VMEM((2, 2, 2, CAP, width), BF16),
            pltpu.VMEM((2, 2, CAP, width), BF16),
            pltpu.VMEM((2, 2, CAP, width), BF16),
            pltpu.VMEM((2, 2, rows, TILE), BF16),
            pltpu.VMEM((2, 3, TILE, TILE), F32),
            dma((3,)),
            dma((4,)),
            dma((4,)),
            dma((2, 2)),
            dma((2, 3)),
            dma((48,)),
            dma((48,)),
            dma((4,)),
            dma((4,)),
            dma((48,)),
            dma((48,)),
            dma((48,)),
            dma((48,)),
            dma((4,)),
            dma((4,)),
        ],
        compiler_params=pltpu.CompilerParams(
            collective_id=0, has_side_effects=True, vmem_limit_bytes=67000000
        ),
        name="layer",
    )(tokens, expert_ids, combine_weights, out_grad, gate_weight, up_weight, down_weight)
    return result[:5]


def solution(mesh):
    in_specs = (
        P("dp", "own"),
        P("dp", None),
        P("dp", None),
        P(None, "own", "dp"),
        P(None, "own", "dp"),
        P(None, "dp", "own"),
        P("dp", "own"),
    )
    out_specs = (
        P("dp", "own"),
        P("dp", "own"),
        P(None, "own", "dp"),
        P(None, "own", "dp"),
        P(None, "dp", "own"),
    )
    return jax.shard_map(local, mesh=mesh, in_specs=in_specs, out_specs=out_specs, check_vma=False)
```

```python
import jax
import jax.numpy as jnp
from jax import lax
from jax.experimental import pallas as pl
from jax.experimental.pallas import tpu as pltpu
from jax.sharding import PartitionSpec as P

CAP = 40
RING = 4
CHUNK = RING * CAP
HALF = CHUNK // 2
TILE = 256
SHARE = 80
MESH = pl.DeviceIdType.MESH
F32 = jnp.float32
BF16 = jnp.bfloat16
MESSAGES = ((0, 1, 0), (1, 1, 0), (0, -1, 0), (1, -1, 0), (0, 1, -1), (1, -1, 1))


def dp_of(z, x, y):
    return z * 8 + x * 4 + y


def place():
    dp, own = lax.axis_index("dp"), lax.axis_index("own")
    z, x, y = dp // 8, (dp // 4) % 2, dp % 4
    core, low = own % 2, own // 2

    def along(axis, step):
        if axis == "y":
            return (dp_of(z, x, (y + step + RING) % RING), own)
        return (dp_of((z + step + RING) % RING, x, y), own)

    partner = (dp_of(z, 1 - x, y), own)
    sibling = (dp, low * 2 + (1 - core))
    across = (dp, (1 - low) * 2 + core)
    return z, x, y, core, along, partner, sibling, across


def send(src, dst, send_sem, recv_sem, device):
    return pltpu.make_async_remote_copy(
        src_ref=src, dst_ref=dst, send_sem=send_sem, recv_sem=recv_sem, device_id=device, device_id_type=MESH
    )


def meet(devices):
    barrier = pltpu.get_barrier_semaphore()
    for device in devices:
        pl.semaphore_signal(barrier, inc=1, device_id=device, device_id_type=MESH)
    return barrier, len(devices)


def nt(a, b):
    return lax.dot_general(a, b, (((1,), (1,)), ((), ())), preferred_element_type=F32)


def nn(a, b):
    return jnp.dot(a, b, preferred_element_type=F32)


def tn(a, b):
    return lax.dot_general(a, b, (((0,), (0,)), ((), ())), preferred_element_type=F32)


def layer_kernel(
    tok, ids, mix, grad, wg_h, wu_h, wd_h,
    mixed, token_grad, dg_h, du_h, dd_h, x_all,
    mine, hot, wg, wu, wd, xin, part, r1, s1, r2, act,
    pb, rd, rb, s2, td, tb, ts, x3, rx3, win, wout,
    load_sem, put_sem, xin_sem, win_sem, wout_sem,
    ag_send, ag_recv, sh_send, sh_recv, x_send, x_recv, own_send, own_recv, c_send, c_recv, y_send, y_recv,
):
    z, x, y, core, along, partner, sibling, across = place()
    first, second = ("y", "z"), ("z", "y")
    coord = {"y": y, "z": z}
    width = wd.shape[-1]
    tiles = width // TILE
    loads = [
        pltpu.make_async_copy(src, dst, load_sem.at[i])
        for i, (src, dst) in enumerate(((wg_h, wg), (wu_h, wu), (wd_h, wd)))
    ]
    for load in loads:
        load.start()
    barrier, count = meet(
        (along("y", 1), along("y", -1), along("z", 1), along("z", -1), partner, sibling, across)
    )
    shard = tok.shape[0]
    earlier = lax.broadcasted_iota(jnp.int32, (shard, shard), 1) < lax.broadcasted_iota(
        jnp.int32, (shard, shard), 0
    )
    slots = lax.broadcasted_iota(jnp.int32, (shard, CAP), 1).astype(F32)
    weight = []
    for e in range(2):
        chosen = (ids[...] == e).astype(F32)
        routed = jnp.sum(chosen, axis=1, keepdims=True)
        weight.append(jnp.sum(chosen * mix[...], axis=1, keepdims=True))
        spread = jnp.broadcast_to(routed, (shard, 128)).astype(BF16)
        position = nn(earlier.astype(F32).astype(BF16), spread)[:, 0:1]
        hot[e] = jnp.where((routed > 0.0) & (position == slots), 1.0, 0.0).astype(BF16)
        mine[0, e] = tn(hot[e], tok[...]).astype(BF16)
        mine[1, e] = tn(hot[e], (weight[e] * grad[...].astype(F32)).astype(BF16)).astype(BF16)
    pl.semaphore_wait(barrier, count)

    def plane(wave):
        return x if wave == 0 else 1 - x

    def q_of(e):
        return z + e * (y - z)

    def piece(t, e, xs, qc, pc):
        row = pl.multiple_of((xs * 16 + qc * 4 + pc) * CAP, 8)
        return x_all.at[t, e, pl.ds(row, CAP)]

    def chunk(t, e, xs, qc, begin=0, end=CHUNK):
        row = pl.multiple_of((xs * 4 + qc) * CHUNK + begin, 16)
        return x_all.at[t, e, pl.ds(row, end - begin)]

    def phase(wave, e, stage, m, arriving=False):
        t, way, shift = MESSAGES[m]
        axis = (first if stage == 0 else second)[e]
        a, b, xs = coord[first[e]], coord[second[e]], plane(wave)
        begin = 0
        if wave == 1 and stage == 1:
            t = 1 - t
            begin = SHARE if m in (1, 2) else 0
        if arriving:
            shift = shift - way
        if stage == 0:
            ref = piece(t, e, xs, b, (a + shift + RING) % RING)
            src = mine.at[t, e] if wave == 0 and m < 4 and not arriving else ref
        else:
            ref = chunk(t, e, xs, (b + shift + RING) % RING, begin)
            src = ref
        index = ((wave * 2 + e) * 2 + stage) * 6 + m
        return send(src, ref, ag_send.at[index], ag_recv.at[index], along(axis, way))

    def share(t, e, arriving=False):
        near = (coord[second[e]] + (-1, 1)[t] + RING) % RING
        ref = chunk(t, e, 1 - x if arriving else x, near, 0, SHARE)
        i = t * 2 + e
        return send(ref, ref, sh_send.at[i], sh_recv.at[i], partner)

    def start(wave, stage, messages):
        for m in messages:
            for e in range(2):
                phase(wave, e, stage, m).start()

    def arrive(wave, stage, messages):
        for m in messages:
            for e in range(2):
                phase(wave, e, stage, m, True).wait_recv()

    def relay(wave, stage):
        for came, out in ((0, 4), (3, 5)):
            arrive(wave, stage, (came,))
            start(wave, stage, (out,))

    puts, crossings, landings = [], [], []
    for t in range(2):
        for e in range(2):
            a, b, i = coord[first[e]], coord[second[e]], t * 2 + e
            puts.append(pltpu.make_async_copy(mine.at[t, e], piece(t, e, x, b, a), put_sem.at[i]))
            crossings.append(send(mine.at[t, e], piece(t, e, x, b, a), x_send.at[i], x_recv.at[i], partner))
            theirs = piece(t, e, 1 - x, b, a)
            landings.append(send(mine.at[t, e], theirs, x_send.at[i], x_recv.at[i], partner))

    steps = [(wave, shift) for wave in range(2) for shift in (0, -1, 1, 2)]

    def row_of(e, wave, shift):
        return (plane(wave) * 4 + (q_of(e) + shift + RING) % RING) * CHUNK

    def own_one(step, e):
        i = step * 2 + e
        far = pl.multiple_of((1 - core) * HALF, HALF)
        return send(part.at[i, :, pl.ds(far, HALF)], r1.at[i], own_send.at[i], own_recv.at[i], sibling)

    def own_two(step, e):
        i = step * 2 + e
        return send(s1.at[i], r2.at[i], own_send.at[16 + i], own_recv.at[16 + i], across)

    def own_three(step, e, arriving=False):
        i = step * 2 + e
        wave, shift = steps[step]
        side = 1 - core if arriving else core
        row = pl.multiple_of(row_of(e, wave, shift) + side * HALF, 16)
        ref = act.at[:, e, pl.ds(row, HALF)]
        return send(ref, ref, own_send.at[32 + i], own_recv.at[32 + i], sibling)

    def fetch(step):
        wave, shift = steps[step]
        return [
            pltpu.make_async_copy(
                chunk(t, e, plane(wave), (q_of(e) + shift + RING) % RING), xin.at[t, e], xin_sem.at[t * 2 + e]
            )
            for t in range(2)
            for e in range(2)
        ]

    def matmuls(step):
        def one(e, carry):
            i = step * 2 + e
            part[i, 0] = nn(xin[0, e], wg[e]).astype(BF16)
            part[i, 1] = nn(xin[0, e], wu[e]).astype(BF16)
            part[i, 2] = nt(xin[1, e], wd[e]).astype(BF16)
            own_one(step, e).start()
            return carry

        lax.fori_loop(0, 2, one, 0)

    def halves(step):
        def one(e, carry):
            i = step * 2 + e
            own_one(step, e).wait_recv()
            near = pl.multiple_of(core * HALF, HALF)
            for k in range(3):
                total = part[i, k, pl.ds(near, HALF), :].astype(F32) + r1[i, k].astype(F32)
                s1[i, k] = total.astype(BF16)
            own_two(step, e).start()
            return carry

        lax.fori_loop(0, 2, one, 0)

    def gates(step):
        wave, shift = steps[step]

        def one(e, carry):
            i = step * 2 + e
            own_two(step, e).wait_recv()
            row = pl.multiple_of(row_of(e, wave, shift) + core * HALF, 16)
            gate = s1[i, 0].astype(F32) + r2[i, 0].astype(F32)
            up = s1[i, 1].astype(F32) + r2[i, 1].astype(F32)
            back = s1[i, 2].astype(F32) + r2[i, 2].astype(F32)
            sigma = jax.nn.sigmoid(gate)
            swish = gate * sigma
            act[0, e, pl.ds(row, HALF), :] = (swish * up).astype(BF16)
            act[1, e, pl.ds(row, HALF), :] = (back * up * sigma * (1.0 + gate * (1.0 - sigma))).astype(BF16)
            act[2, e, pl.ds(row, HALF), :] = (back * swish).astype(BF16)
            own_three(step, e).start()
            return carry

        lax.fori_loop(0, 2, one, 0)

    def compute(step):
        copies = fetch(step)
        for copy in copies:
            copy.start()
        if step >= 2:
            gates(step - 2)
        for copy in copies:
            copy.wait()
        matmuls(step)
        if step >= 1:
            halves(step - 1)

    def settled(group):
        for step in group:
            for e in range(2):
                own_three(step, e, True).wait_recv()

    def hop(side, e, stage, m):
        t = m % 2
        way = (1, -1, 1, -1, -1, 1)[m]
        axis = (second if stage == 0 else first)[e]
        index = ((side * 2 + e) * 2 + stage) * 6 + m
        if stage == 0:
            src = pb.at[side, (3, 3, 1, 2, 2, 1)[m], t, e]
            dst = rd.at[side, t, e] if m < 2 else rb.at[side, (m - 2) // 2, t, e]
        else:
            a = coord[first[e]]
            far = s2.at[side, t, e, (a + 2) % RING]
            near = s2.at[side, t, e, (a + way + RING) % RING]
            src = far if m < 2 else ts.at[side, t, e] if m < 4 else near
            dst = td.at[side, t, e] if m < 2 else tb.at[side, (m - 2) // 2, t, e]
        return send(src, dst, c_send.at[index], c_recv.at[index], along(axis, way))

    def go(side, stage, messages):
        for m in messages:
            for e in range(2):
                hop(side, e, stage, m).start()

    def come(side, stage, messages):
        for m in messages:
            for e in range(2):
                hop(side, e, stage, m).wait_recv()

    def over_tiles(one):
        def step(i, carry):
            e, n = i // tiles, i % tiles
            one(e, pl.ds(pl.multiple_of(n * TILE, TILE), TILE))
            return carry

        lax.fori_loop(0, 2 * tiles, step, 0)

    def produce(side, j):
        shift = (0, 1, -1, 2)[j]

        def one(e, col):
            rows = pl.ds(pl.multiple_of(row_of(e, 1 - side, shift), 32), CHUNK)
            pb[side, j, 0, e, :, col] = nn(act[0, e, rows, :], wd[e, :, col]).astype(BF16)
            back = nt(act[1, e, rows, :], wg[e, col, :]) + nt(act[2, e, rows, :], wu[e, col, :])
            pb[side, j, 1, e, :, col] = back.astype(BF16)

        over_tiles(one)

    def relay_first(side):
        for t in range(2):
            come(side, 0, (t,))

            def one(e, col):
                total = pb[side, 1 + t, t, e, :, col].astype(F32) + rd[side, t, e, :, col].astype(F32)
                pb[side, 1 + t, t, e, :, col] = total.astype(BF16)

            over_tiles(one)
            go(side, 0, (2 + t,))

    def gather_first(side):
        come(side, 0, (2, 3, 4, 5))
        for t in range(2):

            def one(e, col):
                total = (
                    pb[side, 0, t, e, :, col].astype(F32)
                    + rb[side, 0, t, e, :, col].astype(F32)
                    + rb[side, 1, t, e, :, col].astype(F32)
                )
                for k in range(RING):
                    s2[side, t, e, k, :, col] = total[k * CAP : (k + 1) * CAP].astype(BF16)

            over_tiles(one)
        go(side, 1, (0, 1, 4, 5))

    def relay_second(side):
        for t in range(2):
            come(side, 1, (t,))
            for e in range(2):
                a = coord[first[e]]
                near = (a + (1, -1)[t] + RING) % RING
                total = s2[side, t, e, near].astype(F32) + td[side, t, e].astype(F32)
                ts[side, t, e] = total.astype(BF16)
            go(side, 1, (2 + t,))

    def total_second(side, t, e):
        a = coord[first[e]]
        return (
            s2[side, t, e, a].astype(F32)
            + tb[side, 0, t, e].astype(F32)
            + tb[side, 1, t, e].astype(F32)
        )

    def crossing(t, e):
        i = t * 2 + e
        return send(x3.at[t, e], rx3.at[t, e], y_send.at[i], y_recv.at[i], partner)

    def weight_in(i, slot):
        e, n = i // tiles, i % tiles
        col = pl.ds(pl.multiple_of(n * TILE, TILE), TILE)
        return [
            pltpu.make_async_copy(x_all.at[t, e, :, col], win.at[slot, t], win_sem.at[slot, t]) for t in range(2)
        ]

    def weight_out(i, slot):
        e, n = i // tiles, i % tiles
        col = pl.ds(pl.multiple_of(n * TILE, TILE), TILE)
        return [
            pltpu.make_async_copy(wout.at[slot, 0], dg_h.at[e, col], wout_sem.at[slot, 0]),
            pltpu.make_async_copy(wout.at[slot, 1], du_h.at[e, col], wout_sem.at[slot, 1]),
            pltpu.make_async_copy(wout.at[slot, 2], dd_h.at[e, :, col], wout_sem.at[slot, 2]),
        ]

    last = 2 * tiles

    def weight_grads(begin, end):
        def step(i, carry):
            slot = i % 2
            for copy in weight_in(i, slot):
                copy.wait()

            @pl.when(i + 1 < last)
            def _():
                for copy in weight_in(i + 1, 1 - slot):
                    copy.start()

            @pl.when(i >= 2)
            def _():
                for copy in weight_out(i - 2, slot):
                    copy.wait()

            e = i // tiles
            wout[slot, 0] = tn(win[slot, 0], act[1, e])
            wout[slot, 1] = tn(win[slot, 0], act[2, e])
            wout[slot, 2] = tn(act[0, e], win[slot, 1])
            for copy in weight_out(i, slot):
                copy.start()
            return carry

        lax.fori_loop(begin, end, step, 0)

    order = (0, 3, 1, 2)
    start(0, 0, order)
    for copy in crossings + puts:
        copy.start()
    relay(0, 0)
    arrive(0, 0, (1, 2, 4, 5))
    for copy in puts:
        copy.wait()
    start(0, 1, (0, 3))
    for copy in landings:
        copy.wait_recv()
    start(1, 0, order)
    start(0, 1, (1, 2))
    for load in loads:
        load.wait()
    compute(0)
    arrive(0, 1, (0, 3))
    for t in range(2):
        for e in range(2):
            share(t, e).start()
    relay(1, 0)
    start(0, 1, (4, 5))
    arrive(0, 1, (1,))
    compute(1)
    arrive(1, 0, (1, 2, 4, 5))
    start(1, 1, order if SHARE < CHUNK else (0, 3))
    arrive(0, 1, (2,))
    compute(2)
    arrive(0, 1, (4, 5))
    compute(3)
    compute(4)
    relay(1, 1)
    for t, m in ((0, 1), (1, 2)):
        if SHARE < CHUNK:
            arrive(1, 1, (m,))
        for e in range(2):
            share(t, e, True).wait_recv()
        compute(5 + t)
    settled((0, 1, 2, 3))
    produce(1, 3)
    produce(1, 1)
    produce(1, 2)
    produce(1, 0)
    arrive(1, 1, (4, 5))
    go(1, 0, (0, 1, 5, 4))
    compute(7)
    gates(6)
    halves(7)
    for copy in weight_in(0, 0):
        copy.start()
    gates(7)
    settled((4, 5, 6, 7))
    produce(0, 3)
    go(0, 0, (0, 1))
    produce(0, 1)
    go(0, 0, (5,))
    produce(0, 2)
    go(0, 0, (4,))
    produce(0, 0)
    weight_grads(0, 4)
    relay_first(0)
    relay_first(1)
    weight_grads(4, 8)
    gather_first(0)
    weight_grads(8, last)
    gather_first(1)
    relay_second(0)
    come(0, 1, (2, 3, 4, 5))
    for t in range(2):
        for e in range(2):
            x3[t, e] = total_second(0, t, e).astype(BF16)
            crossing(t, e).start()
    relay_second(1)
    come(1, 1, (2, 3, 4, 5))
    final = [[None, None], [None, None]]
    for t in range(2):
        for e in range(2):
            crossing(t, e).wait_recv()
            final[t][e] = (total_second(1, t, e) + rx3[t, e].astype(F32)).astype(BF16)
    mixed[...] = (weight[0] * nn(hot[0], final[0][0]) + weight[1] * nn(hot[1], final[0][1])).astype(BF16)
    token_grad[...] = (nn(hot[0], final[1][0]) + nn(hot[1], final[1][1])).astype(BF16)
    for i in (last - 2, last - 1):
        for copy in weight_out(i, i % 2):
            copy.wait()
    for e in range(2):
        for wave in range(2):
            for stage in range(2):
                for m in range(6):
                    if SHARE < CHUNK or (wave, stage) != (1, 1) or m not in (1, 2):
                        phase(wave, e, stage, m).wait_send()
                    hop(wave, e, stage, m).wait_send()
        for t in range(2):
            crossings[t * 2 + e].wait_send()
            share(t, e).wait_send()
            crossing(t, e).wait_send()
        for step in range(8):
            own_one(step, e).wait_send()
            own_two(step, e).wait_send()
            own_three(step, e).wait_send()


def local(tokens, expert_ids, combine_weights, gate_weight, up_weight, down_weight, out_grad):
    shard, width = tokens.shape
    experts, hidden = gate_weight.shape[0], gate_weight.shape[2]
    rows = 32 * CAP
    vmem = pl.BlockSpec(memory_space=pltpu.VMEM)
    hbm = pl.BlockSpec(memory_space=pl.ANY)
    dma = pltpu.SemaphoreType.DMA
    out = jax.ShapeDtypeStruct((shard, width), BF16)
    result = pl.pallas_call(
        layer_kernel,
        out_shape=(
            out,
            out,
            jax.ShapeDtypeStruct(gate_weight.shape, F32),
            jax.ShapeDtypeStruct(up_weight.shape, F32),
            jax.ShapeDtypeStruct(down_weight.shape, F32),
            jax.ShapeDtypeStruct((2, experts, rows, width), BF16),
        ),
        in_specs=[vmem] * 4 + [hbm] * 3,
        out_specs=(vmem,) * 2 + (hbm,) * 4,
        scratch_shapes=[
            pltpu.VMEM((2, 2, CAP, width), BF16),
            pltpu.VMEM((2, shard, CAP), BF16),
            pltpu.VMEM(gate_weight.shape, BF16),
            pltpu.VMEM(up_weight.shape, BF16),
            pltpu.VMEM(down_weight.shape, BF16),
            pltpu.VMEM((2, 2, CHUNK, width), BF16),
            pltpu.VMEM((16, 3, CHUNK, hidden), BF16),
            pltpu.VMEM((16, 3, HALF, hidden), BF16),
            pltpu.VMEM((16, 3, HALF, hidden), BF16),
            pltpu.VMEM((16, 3, HALF, hidden), BF16),
            pltpu.VMEM((3, 2, rows, hidden), BF16),
            pltpu.VMEM((2, 4, 2, 2, CHUNK, width), BF16),
            pltpu.VMEM((2, 2, 2, CHUNK, width), BF16),
            pltpu.VMEM((2, 2, 2, 2, CHUNK, width), BF16),
            pltpu.VMEM((2, 2, 2, RING, CAP, width), BF16),
            pltpu.VMEM((2, 2, 2, CAP, width), BF16),
            pltpu.VMEM((2, 2, 2, 2, CAP, width), BF16),
            pltpu.VMEM((2, 2, 2, CAP, width), BF16),
            pltpu.VMEM((2, 2, CAP, width), BF16),
            pltpu.VMEM((2, 2, CAP, width), BF16),
            pltpu.VMEM((2, 2, rows, TILE), BF16),
            pltpu.VMEM((2, 3, TILE, TILE), F32),
            dma((3,)),
            dma((4,)),
            dma((4,)),
            dma((2, 2)),
            dma((2, 3)),
            dma((48,)),
            dma((48,)),
            dma((4,)),
            dma((4,)),
            dma((4,)),
            dma((4,)),
            dma((48,)),
            dma((48,)),
            dma((48,)),
            dma((48,)),
            dma((4,)),
            dma((4,)),
        ],
        compiler_params=pltpu.CompilerParams(
            collective_id=0, has_side_effects=True, vmem_limit_bytes=67000000
        ),
        name="layer",
    )(tokens, expert_ids, combine_weights, out_grad, gate_weight, up_weight, down_weight)
    return result[:5]


def solution(mesh):
    in_specs = (
        P("dp", "own"),
        P("dp", None),
        P("dp", None),
        P(None, "own", "dp"),
        P(None, "own", "dp"),
        P(None, "dp", "own"),
        P("dp", "own"),
    )
    out_specs = (
        P("dp", "own"),
        P("dp", "own"),
        P(None, "own", "dp"),
        P(None, "own", "dp"),
        P(None, "dp", "own"),
    )
    return jax.shard_map(local, mesh=mesh, in_specs=in_specs, out_specs=out_specs, check_vma=False)
```

```python
import jax
import jax.numpy as jnp
from jax import lax
from jax.experimental import pallas as pl
from jax.experimental.pallas import tpu as pltpu
from jax.sharding import PartitionSpec as P

CAP = 40
RING = 4
CHUNK = RING * CAP
HALF = CHUNK // 2
TILE = 256
SHARE = 80
MESH = pl.DeviceIdType.MESH
F32 = jnp.float32
BF16 = jnp.bfloat16
MESSAGES = ((0, 1, 0), (1, 1, 0), (0, -1, 0), (1, -1, 0), (0, 1, -1), (1, -1, 1))


def dp_of(z, x, y):
    return z * 8 + x * 4 + y


def place():
    dp, own = lax.axis_index("dp"), lax.axis_index("own")
    z, x, y = dp // 8, (dp // 4) % 2, dp % 4
    core, low = own % 2, own // 2

    def along(axis, step):
        if axis == "y":
            return (dp_of(z, x, (y + step + RING) % RING), own)
        return (dp_of((z + step + RING) % RING, x, y), own)

    partner = (dp_of(z, 1 - x, y), own)
    sibling = (dp, low * 2 + (1 - core))
    across = (dp, (1 - low) * 2 + core)
    return z, x, y, core, along, partner, sibling, across


def send(src, dst, send_sem, recv_sem, device):
    return pltpu.make_async_remote_copy(
        src_ref=src, dst_ref=dst, send_sem=send_sem, recv_sem=recv_sem, device_id=device, device_id_type=MESH
    )


def meet(devices):
    barrier = pltpu.get_barrier_semaphore()
    for device in devices:
        pl.semaphore_signal(barrier, inc=1, device_id=device, device_id_type=MESH)
    return barrier, len(devices)


def nt(a, b):
    return lax.dot_general(a, b, (((1,), (1,)), ((), ())), preferred_element_type=F32)


def nn(a, b):
    return jnp.dot(a, b, preferred_element_type=F32)


def tn(a, b):
    return lax.dot_general(a, b, (((0,), (0,)), ((), ())), preferred_element_type=F32)


def layer_kernel(
    tok, ids, mix, grad, wg_h, wu_h, wd_h,
    mixed, token_grad, dg_h, du_h, dd_h, x_all,
    mine, hot, wg, wu, wd, xin, part, r1, s1, r2, act,
    pb, rd, rb, s2, td, tb, ts, x3, rx3, win, wout,
    load_sem, put_sem, xin_sem, win_sem, wout_sem,
    ag_send, ag_recv, sh_send, sh_recv, x_send, x_recv, own_send, own_recv, c_send, c_recv, y_send, y_recv,
):
    z, x, y, core, along, partner, sibling, across = place()
    first, second = ("y", "z"), ("z", "y")
    coord = {"y": y, "z": z}
    width = wd.shape[-1]
    tiles = width // TILE
    loads = [
        pltpu.make_async_copy(src, dst, load_sem.at[i])
        for i, (src, dst) in enumerate(((wg_h, wg), (wu_h, wu), (wd_h, wd)))
    ]
    for load in loads:
        load.start()
    barrier, count = meet(
        (along("y", 1), along("y", -1), along("z", 1), along("z", -1), partner, sibling, across)
    )
    shard = tok.shape[0]
    earlier = lax.broadcasted_iota(jnp.int32, (shard, shard), 1) < lax.broadcasted_iota(
        jnp.int32, (shard, shard), 0
    )
    slots = lax.broadcasted_iota(jnp.int32, (shard, CAP), 1).astype(F32)
    weight = []
    for e in range(2):
        chosen = (ids[...] == e).astype(F32)
        routed = jnp.sum(chosen, axis=1, keepdims=True)
        weight.append(jnp.sum(chosen * mix[...], axis=1, keepdims=True))
        spread = jnp.broadcast_to(routed, (shard, 128)).astype(BF16)
        position = nn(earlier.astype(F32).astype(BF16), spread)[:, 0:1]
        hot[e] = jnp.where((routed > 0.0) & (position == slots), 1.0, 0.0).astype(BF16)
        mine[0, e] = tn(hot[e], tok[...]).astype(BF16)
        mine[1, e] = tn(hot[e], (weight[e] * grad[...].astype(F32)).astype(BF16)).astype(BF16)
    pl.semaphore_wait(barrier, count)

    def plane(wave):
        return x if wave == 0 else 1 - x

    def q_of(e):
        return z + e * (y - z)

    def piece(t, e, xs, qc, pc):
        row = pl.multiple_of((xs * 16 + qc * 4 + pc) * CAP, 8)
        return x_all.at[t, e, pl.ds(row, CAP)]

    def chunk(t, e, xs, qc, begin=0, end=CHUNK):
        row = pl.multiple_of((xs * 4 + qc) * CHUNK + begin, 16)
        return x_all.at[t, e, pl.ds(row, end - begin)]

    def phase(wave, e, stage, m, arriving=False):
        t, way, shift = MESSAGES[m]
        axis = (first if stage == 0 else second)[e]
        a, b, xs = coord[first[e]], coord[second[e]], plane(wave)
        begin = 0
        if wave == 1 and stage == 1:
            t = 1 - t
            begin = SHARE if m in (1, 2) else 0
        if arriving:
            shift = shift - way
        if stage == 0:
            ref = piece(t, e, xs, b, (a + shift + RING) % RING)
            src = mine.at[t, e] if wave == 0 and m < 4 and not arriving else ref
        else:
            ref = chunk(t, e, xs, (b + shift + RING) % RING, begin)
            src = ref
        index = ((wave * 2 + e) * 2 + stage) * 6 + m
        return send(src, ref, ag_send.at[index], ag_recv.at[index], along(axis, way))

    def share(t, e, arriving=False):
        near = (coord[second[e]] + (-1, 1)[t] + RING) % RING
        ref = chunk(t, e, 1 - x if arriving else x, near, 0, SHARE)
        i = t * 2 + e
        return send(ref, ref, sh_send.at[i], sh_recv.at[i], partner)

    def start(wave, stage, messages):
        for m in messages:
            for e in range(2):
                phase(wave, e, stage, m).start()

    def arrive(wave, stage, messages):
        for m in messages:
            for e in range(2):
                phase(wave, e, stage, m, True).wait_recv()

    def relay(wave, stage):
        for came, out in ((0, 4), (3, 5)):
            arrive(wave, stage, (came,))
            start(wave, stage, (out,))

    puts, crossings, landings = [], [], []
    for t in range(2):
        for e in range(2):
            a, b, i = coord[first[e]], coord[second[e]], t * 2 + e
            puts.append(pltpu.make_async_copy(mine.at[t, e], piece(t, e, x, b, a), put_sem.at[i]))
            crossings.append(send(mine.at[t, e], piece(t, e, x, b, a), x_send.at[i], x_recv.at[i], partner))
            theirs = piece(t, e, 1 - x, b, a)
            landings.append(send(mine.at[t, e], theirs, x_send.at[i], x_recv.at[i], partner))

    steps = [(wave, shift) for wave in range(2) for shift in (0, -1, 1, 2)]

    def row_of(e, wave, shift):
        return (plane(wave) * 4 + (q_of(e) + shift + RING) % RING) * CHUNK

    def own_one(step, e):
        i = step * 2 + e
        far = pl.multiple_of((1 - core) * HALF, HALF)
        return send(part.at[i, :, pl.ds(far, HALF)], r1.at[i], own_send.at[i], own_recv.at[i], sibling)

    def own_two(step, e):
        i = step * 2 + e
        return send(s1.at[i], r2.at[i], own_send.at[16 + i], own_recv.at[16 + i], across)

    def own_three(step, e, arriving=False):
        i = step * 2 + e
        wave, shift = steps[step]
        side = 1 - core if arriving else core
        row = pl.multiple_of(row_of(e, wave, shift) + side * HALF, 16)
        ref = act.at[:, e, pl.ds(row, HALF)]
        return send(ref, ref, own_send.at[32 + i], own_recv.at[32 + i], sibling)

    def fetch(step):
        wave, shift = steps[step]
        return [
            pltpu.make_async_copy(
                chunk(t, e, plane(wave), (q_of(e) + shift + RING) % RING), xin.at[t, e], xin_sem.at[t * 2 + e]
            )
            for t in range(2)
            for e in range(2)
        ]

    def matmuls(step):
        def one(e, carry):
            i = step * 2 + e
            part[i, 0] = nn(xin[0, e], wg[e]).astype(BF16)
            part[i, 1] = nn(xin[0, e], wu[e]).astype(BF16)
            part[i, 2] = nt(xin[1, e], wd[e]).astype(BF16)
            own_one(step, e).start()
            return carry

        lax.fori_loop(0, 2, one, 0)

    def halves(step):
        def one(e, carry):
            i = step * 2 + e
            own_one(step, e).wait_recv()
            near = pl.multiple_of(core * HALF, HALF)
            for k in range(3):
                total = part[i, k, pl.ds(near, HALF), :].astype(F32) + r1[i, k].astype(F32)
                s1[i, k] = total.astype(BF16)
            own_two(step, e).start()
            return carry

        lax.fori_loop(0, 2, one, 0)

    def gates(step):
        wave, shift = steps[step]

        def one(e, carry):
            i = step * 2 + e
            own_two(step, e).wait_recv()
            row = pl.multiple_of(row_of(e, wave, shift) + core * HALF, 16)
            gate = s1[i, 0].astype(F32) + r2[i, 0].astype(F32)
            up = s1[i, 1].astype(F32) + r2[i, 1].astype(F32)
            back = s1[i, 2].astype(F32) + r2[i, 2].astype(F32)
            sigma = jax.nn.sigmoid(gate)
            swish = gate * sigma
            act[0, e, pl.ds(row, HALF), :] = (swish * up).astype(BF16)
            act[1, e, pl.ds(row, HALF), :] = (back * up * sigma * (1.0 + gate * (1.0 - sigma))).astype(BF16)
            act[2, e, pl.ds(row, HALF), :] = (back * swish).astype(BF16)
            own_three(step, e).start()
            return carry

        lax.fori_loop(0, 2, one, 0)

    def compute(step):
        copies = fetch(step)
        for copy in copies:
            copy.start()
        if step >= 2:
            gates(step - 2)
        for copy in copies:
            copy.wait()
        matmuls(step)
        if step >= 1:
            halves(step - 1)

    def settled(group):
        for step in group:
            for e in range(2):
                own_three(step, e, True).wait_recv()

    def hop(side, e, stage, m):
        t = m % 2
        way = (1, -1, 1, -1, -1, 1)[m]
        axis = (second if stage == 0 else first)[e]
        index = ((side * 2 + e) * 2 + stage) * 6 + m
        if stage == 0:
            src = pb.at[side, (3, 3, 1, 2, 2, 1)[m], t, e]
            dst = rd.at[side, t, e] if m < 2 else rb.at[side, (m - 2) // 2, t, e]
        else:
            a = coord[first[e]]
            far = s2.at[side, t, e, (a + 2) % RING]
            near = s2.at[side, t, e, (a + way + RING) % RING]
            src = far if m < 2 else ts.at[side, t, e] if m < 4 else near
            dst = td.at[side, t, e] if m < 2 else tb.at[side, (m - 2) // 2, t, e]
        return send(src, dst, c_send.at[index], c_recv.at[index], along(axis, way))

    def go(side, stage, messages):
        for m in messages:
            for e in range(2):
                hop(side, e, stage, m).start()

    def come(side, stage, messages):
        for m in messages:
            for e in range(2):
                hop(side, e, stage, m).wait_recv()

    def over_tiles(one):
        def step(i, carry):
            e, n = i // tiles, i % tiles
            one(e, pl.ds(pl.multiple_of(n * TILE, TILE), TILE))
            return carry

        lax.fori_loop(0, 2 * tiles, step, 0)

    def produce(side, j):
        shift = (0, 1, -1, 2)[j]

        def one(e, col):
            rows = pl.ds(pl.multiple_of(row_of(e, 1 - side, shift), 32), CHUNK)
            pb[side, j, 0, e, :, col] = nn(act[0, e, rows, :], wd[e, :, col]).astype(BF16)
            back = nt(act[1, e, rows, :], wg[e, col, :]) + nt(act[2, e, rows, :], wu[e, col, :])
            pb[side, j, 1, e, :, col] = back.astype(BF16)

        over_tiles(one)

    def relay_first(side):
        for t in range(2):
            come(side, 0, (t,))

            def one(e, col):
                total = pb[side, 1 + t, t, e, :, col].astype(F32) + rd[side, t, e, :, col].astype(F32)
                pb[side, 1 + t, t, e, :, col] = total.astype(BF16)

            over_tiles(one)
            go(side, 0, (2 + t,))

    def gather_first(side):
        come(side, 0, (2, 3, 4, 5))
        for t in range(2):

            def one(e, col):
                total = (
                    pb[side, 0, t, e, :, col].astype(F32)
                    + rb[side, 0, t, e, :, col].astype(F32)
                    + rb[side, 1, t, e, :, col].astype(F32)
                )
                for k in range(RING):
                    s2[side, t, e, k, :, col] = total[k * CAP : (k + 1) * CAP].astype(BF16)

            over_tiles(one)
        go(side, 1, (0, 1, 4, 5))

    def relay_second(side):
        for t in range(2):
            come(side, 1, (t,))
            for e in range(2):
                a = coord[first[e]]
                near = (a + (1, -1)[t] + RING) % RING
                total = s2[side, t, e, near].astype(F32) + td[side, t, e].astype(F32)
                ts[side, t, e] = total.astype(BF16)
            go(side, 1, (2 + t,))

    def total_second(side, t, e):
        a = coord[first[e]]
        return (
            s2[side, t, e, a].astype(F32)
            + tb[side, 0, t, e].astype(F32)
            + tb[side, 1, t, e].astype(F32)
        )

    def crossing(t, e):
        i = t * 2 + e
        return send(x3.at[t, e], rx3.at[t, e], y_send.at[i], y_recv.at[i], partner)

    def weight_in(i, slot):
        e, n = i // tiles, i % tiles
        col = pl.ds(pl.multiple_of(n * TILE, TILE), TILE)
        return [
            pltpu.make_async_copy(x_all.at[t, e, :, col], win.at[slot, t], win_sem.at[slot, t]) for t in range(2)
        ]

    def weight_out(i, slot):
        e, n = i // tiles, i % tiles
        col = pl.ds(pl.multiple_of(n * TILE, TILE), TILE)
        return [
            pltpu.make_async_copy(wout.at[slot, 0], dg_h.at[e, col], wout_sem.at[slot, 0]),
            pltpu.make_async_copy(wout.at[slot, 1], du_h.at[e, col], wout_sem.at[slot, 1]),
            pltpu.make_async_copy(wout.at[slot, 2], dd_h.at[e, :, col], wout_sem.at[slot, 2]),
        ]

    last = 2 * tiles

    def weight_grads(begin, end):
        def step(i, carry):
            slot = i % 2
            for copy in weight_in(i, slot):
                copy.wait()

            @pl.when(i + 1 < last)
            def _():
                for copy in weight_in(i + 1, 1 - slot):
                    copy.start()

            @pl.when(i >= 2)
            def _():
                for copy in weight_out(i - 2, slot):
                    copy.wait()

            e = i // tiles
            wout[slot, 0] = tn(win[slot, 0], act[1, e])
            wout[slot, 1] = tn(win[slot, 0], act[2, e])
            wout[slot, 2] = tn(act[0, e], win[slot, 1])
            for copy in weight_out(i, slot):
                copy.start()
            return carry

        lax.fori_loop(begin, end, step, 0)

    order = (0, 3, 1, 2)
    start(0, 0, order)
    for copy in crossings + puts:
        copy.start()
    relay(0, 0)
    arrive(0, 0, (1, 2, 4, 5))
    for copy in puts:
        copy.wait()
    start(0, 1, (0, 3))
    for copy in landings:
        copy.wait_recv()
    start(1, 0, order)
    start(0, 1, (1, 2))
    for load in loads:
        load.wait()
    compute(0)
    arrive(0, 1, (0, 3))
    for t in range(2):
        for e in range(2):
            share(t, e).start()
    relay(1, 0)
    start(0, 1, (4, 5))
    arrive(0, 1, (1,))
    compute(1)
    arrive(1, 0, (1, 2, 4, 5))
    start(1, 1, order if SHARE < CHUNK else (0, 3))
    arrive(0, 1, (2,))
    compute(2)
    arrive(0, 1, (4, 5))
    compute(3)
    compute(4)
    relay(1, 1)
    for t, m in ((0, 1), (1, 2)):
        if SHARE < CHUNK:
            arrive(1, 1, (m,))
        for e in range(2):
            share(t, e, True).wait_recv()
        compute(5 + t)
    settled((0, 1, 2, 3))
    produce(1, 3)
    go(1, 0, (0, 1))
    produce(1, 1)
    go(1, 0, (5,))
    produce(1, 2)
    go(1, 0, (4,))
    produce(1, 0)
    arrive(1, 1, (4, 5))
    compute(7)
    gates(6)
    halves(7)
    for copy in weight_in(0, 0):
        copy.start()
    gates(7)
    settled((4, 5, 6, 7))
    produce(0, 3)
    go(0, 0, (0, 1))
    produce(0, 1)
    go(0, 0, (5,))
    produce(0, 2)
    go(0, 0, (4,))
    produce(0, 0)
    weight_grads(0, 4)
    relay_first(0)
    relay_first(1)
    weight_grads(4, 8)
    gather_first(0)
    weight_grads(8, last)
    gather_first(1)
    relay_second(0)
    come(0, 1, (2, 3, 4, 5))
    for t in range(2):
        for e in range(2):
            x3[t, e] = total_second(0, t, e).astype(BF16)
            crossing(t, e).start()
    relay_second(1)
    come(1, 1, (2, 3, 4, 5))
    final = [[None, None], [None, None]]
    for t in range(2):
        for e in range(2):
            crossing(t, e).wait_recv()
            final[t][e] = (total_second(1, t, e) + rx3[t, e].astype(F32)).astype(BF16)
    mixed[...] = (weight[0] * nn(hot[0], final[0][0]) + weight[1] * nn(hot[1], final[0][1])).astype(BF16)
    token_grad[...] = (nn(hot[0], final[1][0]) + nn(hot[1], final[1][1])).astype(BF16)
    for i in (last - 2, last - 1):
        for copy in weight_out(i, i % 2):
            copy.wait()
    for e in range(2):
        for wave in range(2):
            for stage in range(2):
                for m in range(6):
                    if SHARE < CHUNK or (wave, stage) != (1, 1) or m not in (1, 2):
                        phase(wave, e, stage, m).wait_send()
                    hop(wave, e, stage, m).wait_send()
        for t in range(2):
            crossings[t * 2 + e].wait_send()
            share(t, e).wait_send()
            crossing(t, e).wait_send()
        for step in range(8):
            own_one(step, e).wait_send()
            own_two(step, e).wait_send()
            own_three(step, e).wait_send()


def local(tokens, expert_ids, combine_weights, gate_weight, up_weight, down_weight, out_grad):
    shard, width = tokens.shape
    experts, hidden = gate_weight.shape[0], gate_weight.shape[2]
    rows = 32 * CAP
    vmem = pl.BlockSpec(memory_space=pltpu.VMEM)
    hbm = pl.BlockSpec(memory_space=pl.ANY)
    dma = pltpu.SemaphoreType.DMA
    out = jax.ShapeDtypeStruct((shard, width), BF16)
    result = pl.pallas_call(
        layer_kernel,
        out_shape=(
            out,
            out,
            jax.ShapeDtypeStruct(gate_weight.shape, F32),
            jax.ShapeDtypeStruct(up_weight.shape, F32),
            jax.ShapeDtypeStruct(down_weight.shape, F32),
            jax.ShapeDtypeStruct((2, experts, rows, width), BF16),
        ),
        in_specs=[vmem] * 4 + [hbm] * 3,
        out_specs=(vmem,) * 2 + (hbm,) * 4,
        scratch_shapes=[
            pltpu.VMEM((2, 2, CAP, width), BF16),
            pltpu.VMEM((2, shard, CAP), BF16),
            pltpu.VMEM(gate_weight.shape, BF16),
            pltpu.VMEM(up_weight.shape, BF16),
            pltpu.VMEM(down_weight.shape, BF16),
            pltpu.VMEM((2, 2, CHUNK, width), BF16),
            pltpu.VMEM((16, 3, CHUNK, hidden), BF16),
            pltpu.VMEM((16, 3, HALF, hidden), BF16),
            pltpu.VMEM((16, 3, HALF, hidden), BF16),
            pltpu.VMEM((16, 3, HALF, hidden), BF16),
            pltpu.VMEM((3, 2, rows, hidden), BF16),
            pltpu.VMEM((2, 4, 2, 2, CHUNK, width), BF16),
            pltpu.VMEM((2, 2, 2, CHUNK, width), BF16),
            pltpu.VMEM((2, 2, 2, 2, CHUNK, width), BF16),
            pltpu.VMEM((2, 2, 2, RING, CAP, width), BF16),
            pltpu.VMEM((2, 2, 2, CAP, width), BF16),
            pltpu.VMEM((2, 2, 2, 2, CAP, width), BF16),
            pltpu.VMEM((2, 2, 2, CAP, width), BF16),
            pltpu.VMEM((2, 2, CAP, width), BF16),
            pltpu.VMEM((2, 2, CAP, width), BF16),
            pltpu.VMEM((2, 2, rows, TILE), BF16),
            pltpu.VMEM((2, 3, TILE, TILE), F32),
            dma((3,)),
            dma((4,)),
            dma((4,)),
            dma((2, 2)),
            dma((2, 3)),
            dma((48,)),
            dma((48,)),
            dma((4,)),
            dma((4,)),
            dma((4,)),
            dma((4,)),
            dma((48,)),
            dma((48,)),
            dma((48,)),
            dma((48,)),
            dma((4,)),
            dma((4,)),
        ],
        compiler_params=pltpu.CompilerParams(
            collective_id=0, has_side_effects=True, vmem_limit_bytes=67000000
        ),
        name="layer",
    )(tokens, expert_ids, combine_weights, out_grad, gate_weight, up_weight, down_weight)
    return result[:5]


def solution(mesh):
    in_specs = (
        P("dp", "own"),
        P("dp", None),
        P("dp", None),
        P(None, "own", "dp"),
        P(None, "own", "dp"),
        P(None, "dp", "own"),
        P("dp", "own"),
    )
    out_specs = (
        P("dp", "own"),
        P("dp", "own"),
        P(None, "own", "dp"),
        P(None, "own", "dp"),
        P(None, "dp", "own"),
    )
    return jax.shard_map(local, mesh=mesh, in_specs=in_specs, out_specs=out_specs, check_vma=False)
```
